32 devices in a mesh: vec: 8 (over z, core), rep: 4 (over y, x).
Axes of the slice: x: 2, y: 2, z: 4, core: 2. Of those that a mesh axis runs over, the one named last changes fastest.
Arguments:
- vectors: bfloat16 [1024, 1024], P('vec'), may hold values from 0 to 2
- pivot_index: int32 [4, 8], P('rep'), may hold values from 0 to 1023
Outputs:
- similarity: bfloat16 [7, 32, 1024, 128], P(None, 'rep', 'vec')
The draws below stay inside these ranges and needn't reach their ends.
All inputs are finite; a program needn't handle non-finite values.
Results may differ from the reference program's by a relative error of at most 0.011.
Values may be sent and summed in bfloat16 or wider, within the bound.
A program may use at most 64 MiB of HBM per device.

```python
import math
import jax
import jax.numpy as jnp
from jax import lax

F = 1024
VB = 128
PIV = 8
HALF = 3
WIN = 7
NV = 1024
PIVOTS = 32
N_VEC = 8
N_REP = 4


def plant(array, rng, least, high):
    longest = array.shape.index(max(array.shape))
    spots = []
    for shift in (0, 1):
        where = [jax.random.randint(jax.random.fold_in(rng, axis), (), 0, length) for axis, length in enumerate(array.shape)]
        where[longest] = (where[longest] + shift) % array.shape[longest]
        spots.append(tuple(where))
    return array.at[spots[0]].set(least).at[spots[1]].set(high)


def steps_of(rng, dims, cuts, least, high):
    loudness = 1.0
    for dim, shards_of in cuts:
        steps = jax.random.uniform(jax.random.fold_in(jax.random.fold_in(rng, 6), dim), (shards_of,), jnp.float32, least / len(cuts), high / len(cuts))
        loudness = loudness * jnp.repeat(jnp.exp(steps), dims[dim] // shards_of).reshape((-1,) + (1,) * (len(dims) - 1 - dim))
    return loudness


def setup_inputs(seed: int = 0) -> dict:
    key_of = jax.random.split(jax.random.key(seed), 3)
    return {
        "vectors": jnp.clip(2.0 * jax.random.uniform(key_of[0], (NV, F), jnp.float32) ** steps_of(key_of[0], (NV, F), ((0, 8),), -0.2, 0.2), 0.0, 2.0).astype(jnp.bfloat16),
        "pivot_index": plant(jax.random.randint(key_of[1], (N_REP, PIV), 0, NV), jax.random.fold_in(key_of[1], 1), 0, NV - 1).astype(jnp.int32),
    }


def reference(vectors, pivot_index):
    chosen = pivot_index.reshape(-1).astype(jnp.int32)
    pivots = vectors[chosen]
    centre = lax.optimization_barrier(jnp.sum(pivots.astype(jnp.float32), axis=1)) / F
    blocks = vectors.reshape(N_VEC, VB, F).astype(jnp.float32)
    pair_gram = jnp.stack([jnp.einsum('iaf,ibf->iab', blocks, jnp.roll(blocks, HALF - offset, axis=0), precision=lax.Precision.HIGHEST) for offset in range(WIN)])

    def one_pivot(inputs):
        pivot_row, level = inputs
        scaled = (vectors.astype(jnp.float32) * pivot_row.astype(jnp.float32)[None, :]).astype(jnp.bfloat16)
        scaled = lax.optimization_barrier(scaled)
        scaled_blocks = scaled.reshape(N_VEC, VB, F).astype(jnp.float32)
        pieces = []
        for offset in range(WIN):
            triple = jnp.einsum('iaf,ibf->iab', scaled_blocks, jnp.roll(blocks, HALF - offset, axis=0), precision=lax.Precision.HIGHEST)
            pieces.append(((triple - level * pair_gram[offset]) / math.sqrt(F)).astype(jnp.bfloat16))
        return jnp.stack(pieces)
    result = lax.map(one_pivot, (pivots, centre))
    return result.reshape(PIVOTS, WIN, NV, VB).transpose(1, 0, 2, 3)
```

```python
import functools
import math

import jax
import jax.numpy as jnp
from jax import lax
from jax.experimental import pallas as pl
from jax.experimental.pallas import tpu as pltpu
from jax.sharding import PartitionSpec as P

HALF = 3
NEAR = 2


def contract(left, right):
    return lax.dot_general(
        left, right, (((1,), (1,)), ((), ())), preferred_element_type=jnp.float32
    )


def kernel(
    n_vec, n_a, n_b, vec_ref, index_ref, out_ref, win, rows_ref, heard, scaled,
    z_send, z_recv, d_send, d_recv, r_send, r_recv, p_send, p_recv, c_send, c_recv, own_sem,
):
    block_rows, fields = vec_ref.shape
    count = index_ref.shape[1]
    n_rep = n_a * n_b
    part = block_rows // n_rep
    half = fields // 2
    me = lax.axis_index("vec")
    rep = lax.axis_index("rep")
    a, b = rep // n_b, rep % n_b
    core = me % 2
    partner = me + 1 - 2 * core

    def at_vec(offset):
        return (me + offset + n_vec) % n_vec

    def rep_of(da, db):
        return ((a + da + n_a) % n_a) * n_b + (b + db + n_b) % n_b

    direct = [(0, i) for i in range(1, n_b)] + [(i, 0) for i in range(1, n_a)]
    diagonal = [(i, j) for i in range(1, n_a) for j in range(1, n_b)]

    barrier = pltpu.get_barrier_semaphore()

    def greet(i, carry):
        pl.semaphore_signal(barrier, inc=1, device_id={"vec": (me + i) % n_vec})
        return carry

    lax.fori_loop(1, n_vec, greet, 0, unroll=n_vec <= 16)
    for da, db in direct:
        pl.semaphore_signal(barrier, inc=1, device_id={"rep": rep_of(da, db)})

    own_copy = pltpu.make_async_copy(vec_ref, win.at[0], own_sem)
    own_copy.start()
    wanted = index_ref[...] - me * block_rows
    spots = lax.broadcasted_iota(jnp.int32, (block_rows, count), 0)
    onehot = (spots == wanted).astype(jnp.bfloat16)
    mine = lax.dot_general(
        onehot, vec_ref[...], (((0,), (0,)), ((), ())), preferred_element_type=jnp.float32
    )
    rows_ref[...] = mine.astype(jnp.bfloat16)
    pl.semaphore_wait(barrier, n_vec - 1 + len(direct))

    started = []

    def remote(src, dst, send_sem, recv_sem, device):
        copy = pltpu.make_async_remote_copy(
            src_ref=src, dst_ref=dst, send_sem=send_sem, recv_sem=recv_sem, device_id=device
        )
        copy.start()
        started.append(copy)
        return copy

    own_rows = pl.ds(pl.multiple_of(rep * part, part), part)
    far = 4 * (2 * core - 1)
    z_copies = []
    for s, offset in enumerate((2, -2, far)):
        z_copies.append(
            remote(
                vec_ref.at[own_rows], win.at[2 + s, own_rows], z_send.at[s], z_recv.at[s],
                {"vec": at_vec(offset)},
            )
        )
    partner_own = remote(vec_ref, win.at[1], c_send.at[0], c_recv.at[0], {"vec": partner})

    def pivot_copy(i):
        return pltpu.make_async_remote_copy(
            src_ref=rows_ref, dst_ref=heard.at[i], send_sem=p_send.at[i], recv_sem=p_recv.at[i],
            device_id={"vec": (me + i + 1) % n_vec},
        )

    def send_pivots(i, carry):
        pivot_copy(i).start()
        return carry

    def take_pivots(i, carry):
        pivot_copy(i).wait()
        return carry

    lax.fori_loop(0, n_vec - 1, send_pivots, 0, unroll=n_vec <= 16)

    per_slot = 1 + len(direct) + 2 * len(diagonal)
    across = [[] for _ in range(3)]

    def hand_over(s, rows, columns, number):
        k = 1 + s * per_slot + number
        across[s].append(
            remote(
                win.at[2 + s, rows, columns], win.at[5 + s, rows, columns],
                c_send.at[k], c_recv.at[k], {"vec": partner},
            )
        )

    everything = pl.ds(0, fields)
    first, second = pl.ds(0, half), pl.ds(half, half)

    def rows_from(da, db):
        return pl.ds(pl.multiple_of(rep_of(-da, -db) * part, part), part)

    d_copies = [[] for _ in range(3)]
    for s in range(3):
        z_copies[s].wait_recv()
        for t, (da, db) in enumerate(direct):
            d_copies[s].append(
                remote(
                    win.at[2 + s, own_rows], win.at[2 + s, own_rows],
                    d_send.at[s, t], d_recv.at[s, t], {"rep": rep_of(da, db)},
                )
            )
        hand_over(s, own_rows, everything, 0)

    r_copies = [[] for _ in range(3)]
    for s in range(3):
        for t, (da, db) in enumerate(direct):
            d_copies[s][t].wait_recv()
            rows = rows_from(da, db)
            if da == 0:
                onward = [((i, 0), first, 2 * diagonal.index((i, db))) for i in range(1, n_a)]
            else:
                onward = [((0, j), second, 2 * diagonal.index((da, j)) + 1) for j in range(1, n_b)]
            for (ra, rb), columns, number in onward:
                r_copies[s].append(
                    (
                        number,
                        remote(
                            win.at[2 + s, rows, columns], win.at[2 + s, rows, columns],
                            r_send.at[s, number], r_recv.at[s, number], {"rep": rep_of(ra, rb)},
                        ),
                    )
                )
            hand_over(s, rows, everything, 1 + t)

    lax.fori_loop(0, n_vec - 1, take_pivots, 0, unroll=n_vec <= 16)
    pivots = rows_ref[...].astype(jnp.float32)
    pivots = lax.fori_loop(
        0, n_vec - 1, lambda i, total: total + heard[i].astype(jnp.float32), pivots, unroll=n_vec <= 16
    )
    level = jnp.sum(pivots, axis=1, keepdims=True) / fields
    pivots = pivots - level
    own = vec_ref[...].astype(jnp.float32)
    for k in range(count):
        scaled[k * block_rows:(k + 1) * block_rows, :] = (own * pivots[k:k + 1, :]).astype(jnp.bfloat16)

    root = 1.0 / math.sqrt(fields)

    def compare(slot, width, offsets):
        right = win[slot:slot + width].reshape(width * block_rows, fields)
        value = (contract(scaled[...], right) * root).astype(jnp.bfloat16)
        for i, offset in enumerate(offsets):
            out_ref[HALF + offset] = value[:, i * block_rows:(i + 1) * block_rows].reshape(
                count, block_rows, block_rows
            )

    own_copy.wait()
    partner_own.wait_recv()
    compare(0, 2, (0, 1 - 2 * core))

    for s in range(3):
        for number, copy in sorted(r_copies[s], key=lambda pair: pair[0]):
            copy.wait_recv()
            da, db = diagonal[number // 2]
            hand_over(s, rows_from(da, db), (first, second)[number % 2], 1 + len(direct) + number)

    compare(2, 2, (-2, 2))
    for s in (0, 1):
        for copy in across[s]:
            copy.wait_recv()
    compare(5, 2, (-1 - 2 * core, 3 - 2 * core))
    for copy in across[2]:
        copy.wait_recv()
    compare(7, 1, (6 * core - 3,))
    for copy in started:
        copy.wait_send()


def solution(mesh):
    n_vec, n_rep = mesh.shape["vec"], mesh.shape["rep"]
    n_b = 2 if n_rep % 2 == 0 else 1
    n_a = n_rep // n_b
    assert n_vec % 2 == 0 and n_vec > 2 * HALF

    def step(vectors, pivot_index):
        rows, fields = vectors.shape
        count = pivot_index.shape[1]
        direct = n_a + n_b - 2
        diagonal = (n_a - 1) * (n_b - 1)
        dma = pltpu.SemaphoreType.DMA
        across = 1 + 3 * (1 + direct + 2 * diagonal)
        vmem = pl.BlockSpec(memory_space=pltpu.VMEM)
        return pl.pallas_call(
            functools.partial(kernel, n_vec, n_a, n_b),
            out_shape=jax.ShapeDtypeStruct((2 * HALF + 1, count, rows, rows), jnp.bfloat16),
            in_specs=[vmem, vmem],
            out_specs=vmem,
            scratch_shapes=[
                pltpu.VMEM((8, rows, fields), jnp.bfloat16),
                pltpu.VMEM((count, fields), jnp.bfloat16),
                pltpu.VMEM((n_vec - 1, count, fields), jnp.bfloat16),
                pltpu.VMEM((count * rows, fields), jnp.bfloat16),
                dma((3,)), dma((3,)),
                dma((3, max(direct, 1))), dma((3, max(direct, 1))),
                dma((3, max(2 * diagonal, 1))), dma((3, max(2 * diagonal, 1))),
                dma((n_vec - 1,)), dma((n_vec - 1,)),
                dma((across,)), dma((across,)),
                dma(()),
            ],
            compiler_params=pltpu.CompilerParams(collective_id=0, has_side_effects=True),
        )(vectors, pivot_index)

    return jax.shard_map(
        step, mesh=mesh, in_specs=(P("vec", None), P("rep", None)),
        out_specs=P(None, "rep", "vec", None), check_vma=False,
    )
```

```python
import functools
import math

import jax
import jax.numpy as jnp
from jax import lax
from jax.experimental import pallas as pl
from jax.experimental.pallas import tpu as pltpu
from jax.sharding import PartitionSpec as P

HALF = 3


def contract(left, right):
    return lax.dot_general(
        left, right, (((1,), (1,)), ((), ())), preferred_element_type=jnp.float32
    )


def kernel(
    n_vec, n_a, n_b, vec_ref, index_ref, out_ref, win, wanted_ref, rows_ref, heard, scaled,
    z_send, z_recv, d_send, d_recv, r_send, r_recv, p_send, p_recv, c_send, c_recv, local_sem,
):
    block_rows, fields = vec_ref.shape
    count = index_ref.shape[1]
    n_rep = n_a * n_b
    chips = n_vec // 2
    part = block_rows // n_rep
    half = fields // 2
    me = lax.axis_index("vec")
    rep = lax.axis_index("rep")
    a, b = rep // n_b, rep % n_b
    chip, core = me // 2, me % 2
    partner = me + 1 - 2 * core

    def at_vec(offset):
        return {"vec": (me + offset + n_vec) % n_vec}

    def rep_of(da, db):
        return ((a + da + n_a) % n_a) * n_b + (b + db + n_b) % n_b

    direct = [(0, i) for i in range(1, n_b)] + [(i, 0) for i in range(1, n_a)]
    diagonal = [(i, j) for i in range(1, n_a) for j in range(1, n_b)]
    short = n_vec <= 16

    own_copy = pltpu.make_async_copy(vec_ref, win.at[0], local_sem.at[0])
    index_copy = pltpu.make_async_copy(index_ref, wanted_ref, local_sem.at[1])
    own_copy.start()
    index_copy.start()

    barrier = pltpu.get_barrier_semaphore()

    def greet(i, carry):
        pl.semaphore_signal(barrier, inc=1, device_id=at_vec(2 * i))
        return carry

    lax.fori_loop(1, chips, greet, 0, unroll=short)
    pl.semaphore_signal(barrier, inc=1, device_id={"vec": partner})
    for da, db in direct:
        pl.semaphore_signal(barrier, inc=1, device_id={"rep": rep_of(da, db)})
    own_copy.wait()
    index_copy.wait()
    pl.semaphore_wait(barrier, chips + len(direct))

    def remote(src, dst, send_sem, recv_sem, device):
        return pltpu.make_async_remote_copy(
            src_ref=src, dst_ref=dst, send_sem=send_sem, recv_sem=recv_sem, device_id=device
        )

    started = []

    def start(copy):
        copy.start()
        started.append(copy)

    own_rows = pl.ds(pl.multiple_of(rep * part, part), part)
    far = 4 * (2 * core - 1)
    first_chip = 1 - (chip + chips - 1) // chips
    last_chip = (chip + 1) // chips
    edge = first_chip + last_chip
    outgoing = (last_chip, 1 + edge, 2 - 2 * edge + first_chip)
    order = (first_chip, 1 + edge, 2 - 2 * edge + last_chip)

    def z_copy(s):
        is_far = s // 2
        offset = (2 - 4 * s) * (1 - is_far) + far * is_far
        return remote(
            win.at[0, own_rows], win.at[2 + 2 * s, own_rows], z_send.at[s], z_recv.at[s], at_vec(offset)
        )

    for s in outgoing:
        start(z_copy(s))
    partner_own = remote(win.at[0], win.at[1], c_send.at[0], c_recv.at[0], {"vec": partner})
    start(partner_own)

    wanted = wanted_ref[...] - me * block_rows
    spots = lax.broadcasted_iota(jnp.int32, (block_rows, count), 0)
    onehot = (spots == wanted).astype(jnp.bfloat16)
    mine = lax.dot_general(
        onehot, win[0], (((0,), (0,)), ((), ())), preferred_element_type=jnp.float32
    )
    rows_ref[...] = mine.astype(jnp.bfloat16)

    def rows_out(i):
        return remote(rows_ref, heard.at[i], p_send.at[i], p_recv.at[i], at_vec(2 * i))

    rows_partner = remote(rows_ref, heard.at[0], p_send.at[0], p_recv.at[0], {"vec": partner})

    def rows_across(i):
        k = chips - 1 + i
        return remote(heard.at[i], heard.at[k], p_send.at[k], p_recv.at[k], {"vec": partner})

    def loop(action):
        def body(i, carry):
            action(i)
            return carry

        lax.fori_loop(1, chips, body, 0, unroll=short)

    per_slot = 1 + len(direct) + 2 * len(diagonal)
    everything = pl.ds(0, fields)
    halves = (pl.ds(0, half), pl.ds(half, half))

    def rows_from(da, db):
        return pl.ds(pl.multiple_of(rep_of(-da, -db) * part, part), part)

    def hand(s, number):
        if number == 0:
            rows, columns = own_rows, everything
        elif number <= len(direct):
            rows, columns = rows_from(*direct[number - 1]), everything
        else:
            which = number - 1 - len(direct)
            rows, columns = rows_from(*diagonal[which // 2]), halves[which % 2]
        k = 1 + s * per_slot + number
        return remote(
            win.at[2 + 2 * s, rows, columns], win.at[3 + 2 * s, rows, columns],
            c_send.at[k], c_recv.at[k], {"vec": partner},
        )

    def d_copy(s, t):
        slot = win.at[2 + 2 * s, own_rows]
        return remote(slot, slot, d_send.at[s, t], d_recv.at[s, t], {"rep": rep_of(*direct[t])})

    def r_copy(s, t, hop, number):
        slot = win.at[2 + 2 * s, rows_from(*direct[t]), halves[number % 2]]
        return remote(slot, slot, r_send.at[s, number], r_recv.at[s, number], {"rep": rep_of(*hop)})

    def relays(t):
        da, db = direct[t]
        if da == 0:
            return [((i, 0), 2 * diagonal.index((i, db))) for i in range(1, n_a)]
        return [((0, j), 2 * diagonal.index((da, j)) + 1) for j in range(1, n_b)]

    def after_z(s):
        z_copy(s).wait_recv()
        for t in range(len(direct)):
            start(d_copy(s, t))
        start(hand(s, 0))

    def after_direct(s):
        for t in range(len(direct)):
            d_copy(s, t).wait_recv()
            for hop, number in relays(t):
                start(r_copy(s, t, hop, number))
            start(hand(s, 1 + t))

    def after_relay(s):
        for number in range(2 * len(diagonal)):
            slot = win.at[2 + 2 * s, rows_from(*diagonal[number // 2]), halves[number % 2]]
            remote(
                slot, slot, r_send.at[s, number], r_recv.at[s, number], {"vec": partner}
            ).wait_recv()
            start(hand(s, 1 + len(direct) + number))

    root = 1.0 / math.sqrt(fields)

    def compare(slot):
        right = win[pl.ds(slot, 2)].reshape(2 * block_rows, fields)
        value = (contract(scaled[...], right) * root).astype(jnp.bfloat16)
        shape = (count, block_rows, block_rows)
        return value[:, :block_rows].reshape(shape), value[:, block_rows:].reshape(shape)

    def finish(s):
        for number in range(per_slot):
            hand(s, number).wait_recv()
        is_far = s // 2
        left, right = compare(2 + 2 * s)

        @pl.when(is_far == 0)
        def _():
            out_ref[HALF + (4 * s - 2) * (1 - is_far)] = left

        out_ref[HALF + (4 * s - 1 - 2 * core) * (1 - is_far) + (6 * core - 3) * is_far] = right

    after_z(order[0])
    start(rows_partner)
    loop(lambda i: rows_out(i).start())
    after_z(order[1])
    after_direct(order[0])
    after_z(order[2])
    after_direct(order[1])

    def pass_rows(i):
        rows_out(i).wait_recv()
        rows_across(i).start()

    loop(pass_rows)
    after_direct(order[2])
    after_relay(order[0])

    rows_partner.wait_recv()
    loop(lambda i: rows_across(i).wait_recv())
    pivots = lax.fori_loop(
        0, n_vec - 1, lambda i, total: total + heard[i].astype(jnp.float32),
        rows_ref[...].astype(jnp.float32), unroll=short,
    )
    level = jnp.sum(pivots, axis=1, keepdims=True) / fields
    pivots = pivots - level
    own = win[0].astype(jnp.float32)
    for k in range(count):
        scaled[k * block_rows:(k + 1) * block_rows, :] = (own * pivots[k:k + 1, :]).astype(jnp.bfloat16)

    partner_own.wait_recv()
    left, right = compare(0)
    out_ref[HALF] = left
    out_ref[HALF + 1 - 2 * core] = right
    after_relay(order[1])
    finish(order[0])
    after_relay(order[2])
    finish(order[1])
    finish(order[2])
    for copy in started:
        copy.wait_send()
    loop(lambda i: rows_out(i).wait_send())
    loop(lambda i: rows_across(i).wait_send())


def solution(mesh):
    n_vec, n_rep = mesh.shape["vec"], mesh.shape["rep"]
    n_b = 2 if n_rep % 2 == 0 else 1
    n_a = n_rep // n_b
    assert n_vec % 2 == 0 and n_vec > 2 * HALF

    def step(vectors, pivot_index):
        rows, fields = vectors.shape
        count = pivot_index.shape[1]
        direct = n_a + n_b - 2
        diagonal = (n_a - 1) * (n_b - 1)
        dma = pltpu.SemaphoreType.DMA
        across = 1 + 3 * (1 + direct + 2 * diagonal)
        vmem = pl.BlockSpec(memory_space=pltpu.VMEM)
        hbm = pl.BlockSpec(memory_space=pltpu.HBM)
        return pl.pallas_call(
            functools.partial(kernel, n_vec, n_a, n_b),
            out_shape=jax.ShapeDtypeStruct((2 * HALF + 1, count, rows, rows), jnp.bfloat16),
            in_specs=[hbm, hbm],
            out_specs=vmem,
            scratch_shapes=[
                pltpu.VMEM((8, rows, fields), jnp.bfloat16),
                pltpu.VMEM((1, count), jnp.int32),
                pltpu.VMEM((count, fields), jnp.bfloat16),
                pltpu.VMEM((n_vec - 1, count, fields), jnp.bfloat16),
                pltpu.VMEM((count * rows, fields), jnp.bfloat16),
                dma((3,)), dma((3,)),
                dma((3, max(direct, 1))), dma((3, max(direct, 1))),
                dma((3, max(2 * diagonal, 1))), dma((3, max(2 * diagonal, 1))),
                dma((n_vec - 1,)), dma((n_vec - 1,)),
                dma((across,)), dma((across,)),
                dma((2,)),
            ],
            compiler_params=pltpu.CompilerParams(
                collective_id=0, has_side_effects=True, vmem_limit_bytes=24 * 2**20
            ),
        )(vectors, pivot_index)

    return jax.shard_map(
        step, mesh=mesh, in_specs=(P("vec", None), P("rep", None)),
        out_specs=P(None, "rep", "vec", None), check_vma=False,
    )
```

```python
import functools
import math

import jax
import jax.numpy as jnp
from jax import lax
from jax.experimental import pallas as pl
from jax.experimental.pallas import tpu as pltpu
from jax.sharding import PartitionSpec as P

HALF = 3


def contract(left, right):
    return lax.dot_general(
        left, right, (((1,), (1,)), ((), ())), preferred_element_type=jnp.float32
    )


def kernel(
    n_vec, n_a, n_b, vec_ref, index_ref, out_ref, win, wanted_ref, rows_ref, heard, scaled,
    z_send, z_recv, d_send, d_recv, r_send, r_recv, p_send, p_recv, c_send, c_recv, local_sem,
):
    block_rows, fields = vec_ref.shape
    count = index_ref.shape[1]
    n_rep = n_a * n_b
    chips = n_vec // 2
    part = block_rows // n_rep
    me = lax.axis_index("vec")
    rep = lax.axis_index("rep")
    a, b = rep // n_b, rep % n_b
    chip, core = me // 2, me % 2
    partner = me + 1 - 2 * core

    def at_vec(offset):
        return {"vec": (me + offset + n_vec) % n_vec}

    def rep_of(da, db):
        return ((a + da + n_a) % n_a) * n_b + (b + db + n_b) % n_b

    direct = [(0, i) for i in range(1, n_b)] + [(i, 0) for i in range(1, n_a)]
    diagonal = [(i, j) for i in range(1, n_a) for j in range(1, n_b)]
    short = n_vec <= 16

    own_copy = pltpu.make_async_copy(vec_ref, win.at[0], local_sem.at[0])
    index_copy = pltpu.make_async_copy(index_ref, wanted_ref, local_sem.at[1])
    own_copy.start()
    index_copy.start()

    barrier = pltpu.get_barrier_semaphore()

    def greet(i, carry):
        pl.semaphore_signal(barrier, inc=1, device_id=at_vec(2 * i))
        return carry

    lax.fori_loop(1, chips, greet, 0, unroll=short)
    pl.semaphore_signal(barrier, inc=1, device_id={"vec": partner})
    for da, db in direct:
        pl.semaphore_signal(barrier, inc=1, device_id={"rep": rep_of(da, db)})
    own_copy.wait()
    index_copy.wait()
    pl.semaphore_wait(barrier, chips + len(direct))

    def remote(src, dst, send_sem, recv_sem, device):
        return pltpu.make_async_remote_copy(
            src_ref=src, dst_ref=dst, send_sem=send_sem, recv_sem=recv_sem, device_id=device
        )

    started = []

    def start(copy):
        copy.start()
        started.append(copy)

    own_rows = pl.ds(pl.multiple_of(rep * part, part), part)
    far = 4 * (2 * core - 1)
    first_chip = 1 - (chip + chips - 1) // chips
    last_chip = (chip + 1) // chips
    edge = first_chip + last_chip
    outgoing = (last_chip, 1 + edge, 2 - 2 * edge + first_chip)
    order = (first_chip, 1 + edge, 2 - 2 * edge + last_chip)

    def z_copy(s):
        is_far = s // 2
        offset = (2 - 4 * s) * (1 - is_far) + far * is_far
        return remote(
            win.at[0, own_rows], win.at[2 + 2 * s, own_rows], z_send.at[s], z_recv.at[s], at_vec(offset)
        )

    for s in outgoing:
        start(z_copy(s))
    partner_own = remote(win.at[0], win.at[1], c_send.at[0], c_recv.at[0], {"vec": partner})
    start(partner_own)

    wanted = wanted_ref[...] - me * block_rows
    spots = lax.broadcasted_iota(jnp.int32, (block_rows, count), 0)
    onehot = (spots == wanted).astype(jnp.bfloat16)
    mine = lax.dot_general(
        onehot, win[0], (((0,), (0,)), ((), ())), preferred_element_type=jnp.float32
    )
    rows_ref[...] = mine.astype(jnp.bfloat16)

    def rows_out(i):
        return remote(rows_ref, heard.at[i], p_send.at[i], p_recv.at[i], at_vec(2 * i))

    rows_partner = remote(rows_ref, heard.at[0], p_send.at[0], p_recv.at[0], {"vec": partner})

    def rows_across(i):
        k = chips - 1 + i
        return remote(heard.at[i], heard.at[k], p_send.at[k], p_recv.at[k], {"vec": partner})

    def loop(action):
        def body(i, carry):
            action(i)
            return carry

        lax.fori_loop(1, chips, body, 0, unroll=short)

    per_slot = 1 + len(direct) + 2 * len(diagonal)
    everything = pl.ds(0, fields)

    def rows_from(da, db):
        return pl.ds(pl.multiple_of(rep_of(-da, -db) * part, part), part)

    def half_from(da, db, h):
        start_row = rep_of(-da, -db) * part + h * (part // 2)
        return pl.ds(pl.multiple_of(start_row, part // 2), part // 2)

    def hand(s, number):
        if number == 0:
            rows, columns = own_rows, everything
        elif number <= len(direct):
            rows, columns = rows_from(*direct[number - 1]), everything
        else:
            which = number - 1 - len(direct)
            rows, columns = half_from(*diagonal[which // 2], which % 2), everything
        k = 1 + s * per_slot + number
        return remote(
            win.at[2 + 2 * s, rows, columns], win.at[3 + 2 * s, rows, columns],
            c_send.at[k], c_recv.at[k], {"vec": partner},
        )

    def hand_all(s):
        k = 1 + s * per_slot
        return remote(
            win.at[2 + 2 * s], win.at[3 + 2 * s], c_send.at[k], c_recv.at[k], {"vec": partner}
        )

    def d_copy(s, t):
        slot = win.at[2 + 2 * s, own_rows]
        return remote(slot, slot, d_send.at[s, t], d_recv.at[s, t], {"rep": rep_of(*direct[t])})

    def r_copy(s, t, hop, number):
        slot = win.at[2 + 2 * s, half_from(*direct[t], number % 2)]
        return remote(slot, slot, r_send.at[s, number], r_recv.at[s, number], {"rep": rep_of(*hop)})

    def relays(t):
        da, db = direct[t]
        if da == 0:
            return [((i, 0), 2 * diagonal.index((i, db))) for i in range(1, n_a)]
        return [((0, j), 2 * diagonal.index((da, j)) + 1) for j in range(1, n_b)]

    def after_z(s):
        z_copy(s).wait_recv()
        for t in range(len(direct)):
            start(d_copy(s, t))

    def after_direct(s):
        for t in range(len(direct)):
            d_copy(s, t).wait_recv()
            for hop, number in relays(t):
                start(r_copy(s, t, hop, number))

    def after_relay(s):
        for number in range(2 * len(diagonal)):
            slot = win.at[2 + 2 * s, half_from(*diagonal[number // 2], number % 2)]
            remote(
                slot, slot, r_send.at[s, number], r_recv.at[s, number], {"vec": partner}
            ).wait_recv()
        start(hand_all(s))

    root = 1.0 / math.sqrt(fields)

    def compare(slot):
        right = win[pl.ds(slot, 2)].reshape(2 * block_rows, fields)
        value = (contract(scaled[...], right) * root).astype(jnp.bfloat16)
        shape = (count, block_rows, block_rows)
        return value[:, :block_rows].reshape(shape), value[:, block_rows:].reshape(shape)

    def finish(s):
        hand_all(s).wait_recv()
        is_far = s // 2
        left, right = compare(2 + 2 * s)

        @pl.when(is_far == 0)
        def _():
            out_ref[HALF + (4 * s - 2) * (1 - is_far)] = left

        out_ref[HALF + (4 * s - 1 - 2 * core) * (1 - is_far) + (6 * core - 3) * is_far] = right

    after_z(order[0])
    start(rows_partner)
    loop(lambda i: rows_out(i).start())
    after_z(order[1])
    after_direct(order[0])
    after_z(order[2])
    after_direct(order[1])

    def pass_rows(i):
        rows_out(i).wait_recv()
        rows_across(i).start()

    loop(pass_rows)
    after_direct(order[2])
    after_relay(order[0])

    rows_partner.wait_recv()
    loop(lambda i: rows_across(i).wait_recv())
    pivots = lax.fori_loop(
        0, n_vec - 1, lambda i, total: total + heard[i].astype(jnp.float32),
        rows_ref[...].astype(jnp.float32), unroll=short,
    )
    level = jnp.sum(pivots, axis=1, keepdims=True) / fields
    pivots = pivots - level
    own = win[0].astype(jnp.float32)
    for k in range(count):
        scaled[k * block_rows:(k + 1) * block_rows, :] = (own * pivots[k:k + 1, :]).astype(jnp.bfloat16)

    partner_own.wait_recv()
    left, right = compare(0)
    out_ref[HALF] = left
    out_ref[HALF + 1 - 2 * core] = right
    after_relay(order[1])
    finish(order[0])
    after_relay(order[2])
    finish(order[1])
    finish(order[2])
    for copy in started:
        copy.wait_send()
    loop(lambda i: rows_out(i).wait_send())
    loop(lambda i: rows_across(i).wait_send())


def solution(mesh):
    n_vec, n_rep = mesh.shape["vec"], mesh.shape["rep"]
    n_b = 2 if n_rep % 2 == 0 else 1
    n_a = n_rep // n_b
    assert n_vec % 2 == 0 and n_vec > 2 * HALF

    def step(vectors, pivot_index):
        rows, fields = vectors.shape
        count = pivot_index.shape[1]
        direct = n_a + n_b - 2
        diagonal = (n_a - 1) * (n_b - 1)
        dma = pltpu.SemaphoreType.DMA
        across = 1 + 3 * (1 + direct + 2 * diagonal)
        vmem = pl.BlockSpec(memory_space=pltpu.VMEM)
        hbm = pl.BlockSpec(memory_space=pltpu.HBM)
        return pl.pallas_call(
            functools.partial(kernel, n_vec, n_a, n_b),
            out_shape=pltpu.VMEM((2 * HALF + 1, count, rows, rows), jnp.bfloat16),
            in_specs=[hbm, hbm],
            out_specs=vmem,
            scratch_shapes=[
                pltpu.VMEM((8, rows, fields), jnp.bfloat16),
                pltpu.VMEM((1, count), jnp.int32),
                pltpu.VMEM((count, fields), jnp.bfloat16),
                pltpu.VMEM((n_vec - 1, count, fields), jnp.bfloat16),
                pltpu.VMEM((count * rows, fields), jnp.bfloat16),
                dma((3,)), dma((3,)),
                dma((3, max(direct, 1))), dma((3, max(direct, 1))),
                dma((3, max(2 * diagonal, 1))), dma((3, max(2 * diagonal, 1))),
                dma((n_vec - 1,)), dma((n_vec - 1,)),
                dma((across,)), dma((across,)),
                dma((2,)),
            ],
            compiler_params=pltpu.CompilerParams(
                collective_id=0, has_side_effects=True, vmem_limit_bytes=65_000_000
            ),
        )(vectors, pivot_index)

    return jax.shard_map(
        step, mesh=mesh, in_specs=(P("vec", None), P("rep", None)),
        out_specs=P(None, "rep", "vec", None), check_vma=False,
    )
```

```python
import functools
import math

import jax
import jax.numpy as jnp
from jax import lax
from jax.experimental import pallas as pl
from jax.experimental.pallas import tpu as pltpu
from jax.sharding import PartitionSpec as P

HALF = 3


def contract(left, right):
    return lax.dot_general(
        left, right, (((1,), (1,)), ((), ())), preferred_element_type=jnp.float32
    )


def arrival(chip, chips):
    first_chip = 1 - (chip + chips - 1) // chips
    last_chip = (chip + 1) // chips
    edge = first_chip + last_chip
    return first_chip, last_chip, edge, (first_chip, 1 + edge, 2 - 2 * edge + last_chip)


def places(s, core):
    is_far = s // 2
    own = HALF + (4 * s - 2) * (1 - is_far)
    other = HALF + (4 * s - 1 - 2 * core) * (1 - is_far) + (6 * core - 3) * is_far
    return is_far, own, other


def products(scaled, win, slot, count, block_rows):
    fields = scaled.shape[1]
    right = win[pl.ds(slot, 2)].reshape(2 * block_rows, fields)
    value = (contract(scaled[...], right) * (1.0 / math.sqrt(fields))).astype(jnp.bfloat16)
    shape = (count, block_rows, block_rows)
    return value[:, :block_rows].reshape(shape), value[:, block_rows:].reshape(shape)


def closing(n_vec, held, win, scaled, out_ref, last, sems):
    window, count, block_rows, _ = held.shape
    me = lax.axis_index("vec")
    core = me % 2
    s = arrival(me // 2, n_vec // 2)[3][2]
    is_far, own, other = places(s, core)
    own = own * (1 - is_far) + other * is_far

    def ready(i):
        return pltpu.make_async_copy(held.at[i], out_ref.at[i], sems.at[i])

    def late(i, place):
        return pltpu.make_async_copy(last.at[i], out_ref.at[place], sems.at[window + i])

    for i in range(window):
        pl.when(jnp.logical_and(own != i, other != i))(lambda i=i: ready(i).start())
    left, right = products(scaled, win, 2 + 2 * s, count, block_rows)
    last[0] = left
    last[1] = right
    pl.when(is_far == 0)(lambda: late(0, own).start())
    late(1, other).start()
    for i in range(window):
        pl.when(jnp.logical_and(own != i, other != i))(lambda i=i: ready(i).wait())
    pl.when(is_far == 0)(lambda: late(0, own).wait())
    late(1, other).wait()


def kernel(
    n_vec, n_a, n_b, vec_ref, index_ref, out_ref, win, scaled, wanted_ref, rows_ref, heard,
    z_send, z_recv, d_send, d_recv, r_send, r_recv, p_send, p_recv, c_send, c_recv, local_sem,
):
    block_rows, fields = vec_ref.shape
    count = index_ref.shape[1]
    n_rep = n_a * n_b
    chips = n_vec // 2
    part = block_rows // n_rep
    me = lax.axis_index("vec")
    rep = lax.axis_index("rep")
    a, b = rep // n_b, rep % n_b
    chip, core = me // 2, me % 2
    partner = me + 1 - 2 * core

    def at_vec(offset):
        return {"vec": (me + offset + n_vec) % n_vec}

    def rep_of(da, db):
        return ((a + da + n_a) % n_a) * n_b + (b + db + n_b) % n_b

    direct = [(0, i) for i in range(1, n_b)] + [(i, 0) for i in range(1, n_a)]
    diagonal = [(i, j) for i in range(1, n_a) for j in range(1, n_b)]
    short = n_vec <= 16

    own_copy = pltpu.make_async_copy(vec_ref, win.at[0], local_sem.at[0])
    index_copy = pltpu.make_async_copy(index_ref, wanted_ref, local_sem.at[1])
    own_copy.start()
    index_copy.start()

    barrier = pltpu.get_barrier_semaphore()

    def greet(i, carry):
        pl.semaphore_signal(barrier, inc=1, device_id=at_vec(2 * i))
        return carry

    lax.fori_loop(1, chips, greet, 0, unroll=short)
    pl.semaphore_signal(barrier, inc=1, device_id={"vec": partner})
    for da, db in direct:
        pl.semaphore_signal(barrier, inc=1, device_id={"rep": rep_of(da, db)})
    own_copy.wait()
    index_copy.wait()
    pl.semaphore_wait(barrier, chips + len(direct))

    def remote(src, dst, send_sem, recv_sem, device):
        return pltpu.make_async_remote_copy(
            src_ref=src, dst_ref=dst, send_sem=send_sem, recv_sem=recv_sem, device_id=device
        )

    started = []

    def start(copy):
        copy.start()
        started.append(copy)

    own_rows = pl.ds(pl.multiple_of(rep * part, part), part)
    far = 4 * (2 * core - 1)
    first_chip, last_chip, edge, order = arrival(chip, chips)
    outgoing = (last_chip, 1 + edge, 2 - 2 * edge + first_chip)

    def z_copy(s):
        is_far = s // 2
        offset = (2 - 4 * s) * (1 - is_far) + far * is_far
        return remote(
            win.at[0, own_rows], win.at[2 + 2 * s, own_rows], z_send.at[s], z_recv.at[s], at_vec(offset)
        )

    for s in outgoing:
        start(z_copy(s))
    partner_own = remote(win.at[0], win.at[1], c_send.at[0], c_recv.at[0], {"vec": partner})
    start(partner_own)

    wanted = wanted_ref[...] - me * block_rows
    spots = lax.broadcasted_iota(jnp.int32, (block_rows, count), 0)
    onehot = (spots == wanted).astype(jnp.bfloat16)
    mine = lax.dot_general(
        onehot, win[0], (((0,), (0,)), ((), ())), preferred_element_type=jnp.float32
    )
    rows_ref[...] = mine.astype(jnp.bfloat16)

    def rows_out(i):
        return remote(rows_ref, heard.at[i], p_send.at[i], p_recv.at[i], at_vec(2 * i))

    rows_partner = remote(rows_ref, heard.at[0], p_send.at[0], p_recv.at[0], {"vec": partner})

    def rows_across(i):
        k = chips - 1 + i
        return remote(heard.at[i], heard.at[k], p_send.at[k], p_recv.at[k], {"vec": partner})

    def loop(action):
        def body(i, carry):
            action(i)
            return carry

        lax.fori_loop(1, chips, body, 0, unroll=short)

    per_slot = 1 + len(direct) + 2 * len(diagonal)
    everything = pl.ds(0, fields)

    def rows_from(da, db):
        return pl.ds(pl.multiple_of(rep_of(-da, -db) * part, part), part)

    def half_from(da, db, h):
        start_row = rep_of(-da, -db) * part + h * (part // 2)
        return pl.ds(pl.multiple_of(start_row, part // 2), part // 2)

    def hand(s, number):
        if number == 0:
            rows, columns = own_rows, everything
        elif number <= len(direct):
            rows, columns = rows_from(*direct[number - 1]), everything
        else:
            which = number - 1 - len(direct)
            rows, columns = half_from(*diagonal[which // 2], which % 2), everything
        k = 1 + s * per_slot + number
        return remote(
            win.at[2 + 2 * s, rows, columns], win.at[3 + 2 * s, rows, columns],
            c_send.at[k], c_recv.at[k], {"vec": partner},
        )

    def hand_all(s):
        k = 1 + s * per_slot
        return remote(
            win.at[2 + 2 * s], win.at[3 + 2 * s], c_send.at[k], c_recv.at[k], {"vec": partner}
        )

    def d_copy(s, t):
        slot = win.at[2 + 2 * s, own_rows]
        return remote(slot, slot, d_send.at[s, t], d_recv.at[s, t], {"rep": rep_of(*direct[t])})

    def r_copy(s, t, hop, number):
        slot = win.at[2 + 2 * s, half_from(*direct[t], number % 2)]
        return remote(slot, slot, r_send.at[s, number], r_recv.at[s, number], {"rep": rep_of(*hop)})

    def relays(t):
        da, db = direct[t]
        if da == 0:
            return [((i, 0), 2 * diagonal.index((i, db))) for i in range(1, n_a)]
        return [((0, j), 2 * diagonal.index((da, j)) + 1) for j in range(1, n_b)]

    def after_z(s):
        z_copy(s).wait_recv()
        for t in range(len(direct)):
            start(d_copy(s, t))

    def after_direct(s):
        for t in range(len(direct)):
            d_copy(s, t).wait_recv()
            for hop, number in relays(t):
                start(r_copy(s, t, hop, number))

    def after_relay(s):
        for number in range(2 * len(diagonal)):
            slot = win.at[2 + 2 * s, half_from(*diagonal[number // 2], number % 2)]
            remote(
                slot, slot, r_send.at[s, number], r_recv.at[s, number], {"vec": partner}
            ).wait_recv()
        start(hand_all(s))

    def compare(slot):
        return products(scaled, win, slot, count, block_rows)

    def finish(s):
        hand_all(s).wait_recv()
        is_far, below, above = places(s, core)
        left, right = compare(2 + 2 * s)

        @pl.when(is_far == 0)
        def _():
            out_ref[below] = left

        out_ref[above] = right

    after_z(order[0])
    start(rows_partner)
    loop(lambda i: rows_out(i).start())
    after_z(order[1])
    after_direct(order[0])
    after_z(order[2])
    after_direct(order[1])

    def pass_rows(i):
        rows_out(i).wait_recv()
        rows_across(i).start()

    loop(pass_rows)
    after_direct(order[2])
    after_relay(order[0])

    rows_partner.wait_recv()
    loop(lambda i: rows_across(i).wait_recv())
    pivots = lax.fori_loop(
        0, n_vec - 1, lambda i, total: total + heard[i].astype(jnp.float32),
        rows_ref[...].astype(jnp.float32), unroll=short,
    )
    level = jnp.sum(pivots, axis=1, keepdims=True) / fields
    pivots = pivots - level
    own = win[0].astype(jnp.float32)
    for k in range(count):
        scaled[k * block_rows:(k + 1) * block_rows, :] = (own * pivots[k:k + 1, :]).astype(jnp.bfloat16)

    partner_own.wait_recv()
    left, right = compare(0)
    out_ref[HALF] = left
    out_ref[HALF + 1 - 2 * core] = right
    after_relay(order[1])
    finish(order[0])
    after_relay(order[2])
    finish(order[1])
    hand_all(order[2]).wait_recv()
    for copy in started:
        copy.wait_send()
    loop(lambda i: rows_out(i).wait_send())
    loop(lambda i: rows_across(i).wait_send())


def solution(mesh):
    n_vec, n_rep = mesh.shape["vec"], mesh.shape["rep"]
    n_b = 2 if n_rep % 2 == 0 else 1
    n_a = n_rep // n_b
    assert n_vec % 2 == 0 and n_vec > 2 * HALF

    def step(vectors, pivot_index):
        rows, fields = vectors.shape
        count = pivot_index.shape[1]
        direct = n_a + n_b - 2
        diagonal = (n_a - 1) * (n_b - 1)
        dma = pltpu.SemaphoreType.DMA
        across = 1 + 3 * (1 + direct + 2 * diagonal)
        vmem = pl.BlockSpec(memory_space=pltpu.VMEM)
        hbm = pl.BlockSpec(memory_space=pltpu.HBM)
        held, win, scaled = pl.pallas_call(
            functools.partial(kernel, n_vec, n_a, n_b),
            out_shape=(
                pltpu.VMEM((2 * HALF + 1, count, rows, rows), jnp.bfloat16),
                pltpu.VMEM((8, rows, fields), jnp.bfloat16),
                pltpu.VMEM((count * rows, fields), jnp.bfloat16),
            ),
            in_specs=[hbm, hbm],
            out_specs=(vmem, vmem, vmem),
            scratch_shapes=[
                pltpu.VMEM((1, count), jnp.int32),
                pltpu.VMEM((count, fields), jnp.bfloat16),
                pltpu.VMEM((n_vec - 1, count, fields), jnp.bfloat16),
                dma((3,)), dma((3,)),
                dma((3, max(direct, 1))), dma((3, max(direct, 1))),
                dma((3, max(2 * diagonal, 1))), dma((3, max(2 * diagonal, 1))),
                dma((n_vec - 1,)), dma((n_vec - 1,)),
                dma((across,)), dma((across,)),
                dma((2,)),
            ],
            compiler_params=pltpu.CompilerParams(
                collective_id=0, has_side_effects=True, vmem_limit_bytes=60_800_000
            ),
        )(vectors, pivot_index)
        return pl.pallas_call(
            functools.partial(closing, n_vec),
            out_shape=jax.ShapeDtypeStruct(held.shape, held.dtype),
            in_specs=[vmem, vmem, vmem],
            out_specs=pl.BlockSpec(memory_space=pl.ANY),
            scratch_shapes=[
                pltpu.VMEM((2, *held.shape[1:]), held.dtype), dma((2 * HALF + 3,)),
            ],
            compiler_params=pltpu.CompilerParams(vmem_limit_bytes=24 * 2**20),
        )(held, win, scaled)

    return jax.shard_map(
        step, mesh=mesh, in_specs=(P("vec", None), P("rep", None)),
        out_specs=P(None, "rep", "vec", None), check_vma=False,
    )
```
